256 devices in a mesh: node: 32 (over z_lo, y, x), col: 8 (over z_hi, core).
Axes of the slice: x: 4, y: 4, z: 8 (z_hi: 4, z_lo: 2; z = z_hi * 2 + z_lo), core: 2. Of those that a mesh axis runs over, the one named last changes fastest.
Arguments:
- coefficients: bfloat16 [128, 256, 8192], P('node', None, 'col'), may hold values from -6 to 6
- transfer: bfloat16 [3, 128, 4, 256, 256], P(None, 'node', None, 'col'), may hold values from -0.1875 to 0.1875
Outputs:
- result: bfloat16 [128, 256, 8192], P('node', None, 'col')
The draws below stay inside these ranges and needn't reach their ends.
All inputs are finite; a program needn't handle non-finite values.
Results may differ from the reference program's by a relative error of at most 0.0058.
Values may be sent and summed in bfloat16 or wider, within the bound.
No kernel may reach another device: no remote copies, remote signals or barrier semaphores. Data moves between devices by JAX's collectives and lax.ppermute only.
A program may use at most 64 MiB of HBM per device.

```python
import jax
import jax.numpy as jnp

RANK = 256
LEVELS = 3
NODES = 128
COLS = 8192


def levels(rng, dims, split, smallest, top_value):
    loudness = 1.0
    for position, shards_of in split:
        draws = jax.random.uniform(jax.random.fold_in(jax.random.fold_in(rng, 6), position), (shards_of,), jnp.float32, smallest / len(split), top_value / len(split))
        loudness = loudness * jnp.repeat(jnp.exp(draws), dims[position] // shards_of).reshape((-1,) + (1,) * (len(dims) - 1 - position))
    return loudness


def bell_draw(stream_key, extent, deviation, bound, shards=(), kind=jnp.bfloat16):
    gain = levels(stream_key, extent, shards, -0.22, 0.18) if shards else 1.0
    entries = jax.random.normal(stream_key, extent, jnp.float32) * deviation * gain
    return jnp.minimum(jnp.maximum(entries, -bound), bound).astype(kind)


def setup_inputs(seed: int = 0) -> dict:
    seeds = jax.random.split(jax.random.key(seed), 3)
    coefficients = bell_draw(seeds[0], (NODES, RANK, COLS), 1.0, 6.0, ((0, 32), (2, 8)))
    transfer = bell_draw(seeds[1], (LEVELS, NODES, 4, RANK, RANK), (4 * RANK) ** -0.5, 0.1875, ((1, 32), (3, 8)))
    return {"coefficients": coefficients, "transfer": transfer}


def reference(coefficients, transfer):
    current = coefficients
    for level_index in range(LEVELS):
        stride = 4 ** level_index
        groups_out = NODES // (4 * stride)
        weights_now = transfer[level_index].reshape(groups_out, 4, stride, 4, RANK, RANK).astype(jnp.float32)
        blocks = current.reshape(groups_out, 4, stride, RANK, COLS).astype(jnp.float32)
        mixed = jnp.einsum('adbjrs,ajbsc->adbrc', weights_now, blocks)
        current = mixed.reshape(NODES, RANK, COLS).astype(jnp.bfloat16)
    return current
```

```python
import functools

import jax
import jax.numpy as jnp
from jax import lax
from jax.experimental import pallas as pl
from jax.experimental.pallas import tpu as pltpu
from jax.sharding import Mesh, PartitionSpec as P

CHUNKS = 2
DIGITS = range(4)


def level_kernel(parent_first, order, own_ref, other_ref, *refs):
    children, outs, weights = refs[:-5], refs[-5:-1], refs[-1]
    core = order[0]
    for half, ref in ((core, own_ref), (1 - core, other_ref)):
        for zh in DIGITS:
            rows = pl.ds(pl.multiple_of(64 * zh + 32 * half, 32), 32)
            for s in DIGITS:
                for p in DIGITS:
                    parent, child = order[1 + s], order[5 + p]
                    piece = ref[parent, zh, child] if parent_first else ref[zh, parent, child]
                    weights[s, p, rows, :] = piece
    blocks = [children[0].at[p] for p in DIGITS] if len(children) == 1 else children
    for s in DIGITS:
        total = sum(
            jnp.dot(weights[s, p], blocks[p][...], preferred_element_type=jnp.float32)
            for p in DIGITS
        )
        outs[s][...] = total.astype(outs[s].dtype)


def level(order, own, other, children, parent_first, chunk):
    whole = lambda a: pl.BlockSpec(a.shape, lambda i, o: (0,) * a.ndim)
    if isinstance(children, (list, tuple)):
        width = children[0].shape[1]
        specs, operands = [whole(a) for a in children], list(children)
    else:
        width = children.shape[2] // CHUNKS
        specs = [pl.BlockSpec((4, 256, width), lambda i, o: (0, 0, chunk))]
        operands = [children]
    return pl.pallas_call(
        functools.partial(level_kernel, parent_first),
        grid_spec=pltpu.PrefetchScalarGridSpec(
            num_scalar_prefetch=1,
            grid=(1,),
            in_specs=[whole(own), whole(other)] + specs,
            out_specs=[pl.BlockSpec((256, width), lambda i, o: (0, 0))] * 4,
            scratch_shapes=[pltpu.VMEM((4, 4, 256, 256), jnp.bfloat16)],
        ),
        out_shape=[jax.ShapeDtypeStruct((256, width), jnp.bfloat16)] * 4,
        cost_estimate=pl.CostEstimate(
            flops=2 * 16 * 256 * 256 * width,
            bytes_accessed=2 * (16 * 256 * 256 + 8 * 256 * width),
            transcendentals=0,
        ),
        compiler_params=pltpu.CompilerParams(vmem_limit_bytes=40 * 2**20),
    )(order, own, other, *operands)


def place_kernel(chunk, width, order, *refs):
    blocks, out, sems = refs[:4], refs[-2], refs[-1]
    copies = [
        pltpu.make_async_copy(
            blocks[s], out.at[order[s], :, pl.ds(chunk * width, width)], sems.at[s]
        )
        for s in DIGITS
    ]
    for copy in copies:
        copy.start()
    for copy in copies:
        copy.wait()


def place(order, blocks, chunk, into):
    width = blocks[0].shape[1]
    extra = [] if into is None else [into]
    anywhere = pl.BlockSpec(memory_space=pl.ANY)
    return pl.pallas_call(
        functools.partial(place_kernel, chunk, width),
        grid_spec=pltpu.PrefetchScalarGridSpec(
            num_scalar_prefetch=1,
            grid=(1,),
            in_specs=[anywhere] * (4 + len(extra)),
            out_specs=anywhere,
            scratch_shapes=[pltpu.SemaphoreType.DMA((4,))],
        ),
        out_shape=jax.ShapeDtypeStruct((4, 256, CHUNKS * width), jnp.bfloat16),
        input_output_aliases={} if into is None else {5: 0},
    )(order, *blocks, *extra)


def shift(array, axis, by):
    size = lax.axis_size(axis)
    return lax.ppermute(array, axis, [(i, (i + by) % size) for i in range(size)])


def swap(array):
    return shift(array, "core", 1)


def gather_weights(shard, axis):
    if axis is None:
        spread = jnp.broadcast_to(shard[None], (4,) + shard.shape)
        got = lax.all_to_all(spread, "zh", 0, 0, tiled=True)
    else:
        spread = jnp.broadcast_to(shard[:, None], (4, 4) + shard.shape[1:])
        got = lax.all_to_all(
            spread.reshape((16,) + shard.shape[1:]), (axis, "zh"), 0, 0, tiled=True
        ).reshape(spread.shape)
    return got, swap(got)


def exchange(blocks, axis):
    return [blocks[0]] + [shift(blocks[s], axis, s) for s in (1, 2, 3)]


def turn(blocks):
    pairs = lambda s: [(4 * b + a, 4 * a + (a + b + s) % 4) for b in DIGITS for a in DIGITS]
    return [lax.ppermute(blocks[s], ("y", "x"), pairs(s)) for s in DIGITS]


def local(coefficients, transfer):
    a, b, core = lax.axis_index("x"), lax.axis_index("y"), lax.axis_index("core")
    steps = jnp.arange(4, dtype=jnp.int32)

    def order(parents, children):
        return jnp.concatenate([core[None], parents % 4, children % 4]).astype(jnp.int32)

    order0 = order(a + steps, steps)
    order1 = order(a + b + steps, a - steps + 4)
    order2 = order(b + steps, a - b - steps + 8)
    orderp = ((b - steps + 4) % 4).astype(jnp.int32)

    w0 = gather_weights(transfer[0], None)
    w1 = gather_weights(transfer[1], "x")
    w2 = gather_weights(transfer[2], "y")
    states = [exchange(level(order0, *w0, coefficients, False, c), "x") for c in range(CHUNKS)]
    states = [turn(level(order1, *w1, s, True, 0)) for s in states]
    states = [exchange(level(order2, *w2, s, True, 0), "y") for s in states]
    result = None
    for c in range(CHUNKS):
        result = place(orderp, states[c], c, result)
    return result


def solution(mesh):
    fine = Mesh(mesh.devices.reshape(2, 4, 4, 4, 2), ("zl", "y", "x", "zh", "core"))
    node, col = ("zl", "y", "x"), ("zh", "core")
    return jax.shard_map(
        local,
        mesh=fine,
        in_specs=(P(node, None, col), P(None, node, None, col, None)),
        out_specs=P(node, None, col),
        check_vma=False,
    )
```

```python
import functools

import jax
import jax.numpy as jnp
from jax import lax
from jax.experimental import pallas as pl
from jax.experimental.pallas import tpu as pltpu
from jax.sharding import Mesh, PartitionSpec as P

DIGITS = range(4)
CHUNKS = 2
VMEM, ALL_VMEM = 20 * 2**20, 60 * 2**20


def assemble(pieces, order, held, weights):
    core, own_zh = order[0], order[1]
    for (behind, other), ref in zip(pieces, held):
        half = 1 - core if other else core
        at = lax.rem(own_zh - behind + 4, 4)
        rows = pl.ds(pl.multiple_of(64 * at + 32 * half, 32), 32)
        weights[:, :, rows, :] = ref[...]


def level_kernel(pieces, order, *refs):
    if pieces:
        held, refs, weights = refs[: len(pieces)], refs[len(pieces) : -1], refs[-1]
        assemble(pieces, order, held, weights)
    else:
        weights, refs = refs[0], refs[1:]
    children, outs = refs[:-4], refs[-4:]
    blocks = [children[0].at[order[6 + p]] for p in DIGITS] if len(children) == 1 else children
    for s in DIGITS:
        total = sum(
            jnp.dot(
                weights[order[2 + s], order[6 + p]],
                blocks[p][...],
                preferred_element_type=jnp.float32,
            )
            for p in DIGITS
        )
        outs[s][...] = total.astype(outs[s].dtype)


def level(order, held, children, pieces=(), chunk=None, vmem=VMEM):
    whole = lambda a: pl.BlockSpec(a.shape, lambda i, o: (0,) * a.ndim)
    operands = list(held) + list(children)
    width = children[0].shape[-1]
    specs = [whole(a) for a in operands]
    if chunk is not None:
        width //= CHUNKS
        specs[-1] = pl.BlockSpec((4, 256, width), lambda i, o: (0, 0, chunk))
    return pl.pallas_call(
        functools.partial(level_kernel, pieces),
        grid_spec=pltpu.PrefetchScalarGridSpec(
            num_scalar_prefetch=1,
            grid=(1,),
            in_specs=specs,
            out_specs=[pl.BlockSpec((256, width), lambda i, o: (0, 0))] * 4,
            scratch_shapes=[pltpu.VMEM((4, 4, 256, 256), jnp.bfloat16)] if pieces else [],
        ),
        out_shape=[jax.ShapeDtypeStruct((256, width), jnp.bfloat16)] * 4,
        cost_estimate=pl.CostEstimate(
            flops=2 * 16 * 256 * 256 * width,
            bytes_accessed=2 * (16 * 256 * 256 + 8 * 256 * width),
            transcendentals=0,
        ),
        compiler_params=pltpu.CompilerParams(vmem_limit_bytes=vmem),
    )(order, *operands)


def place_kernel(order, *refs):
    blocks, out = refs[:4], refs[-1]
    for s in DIGITS:
        @pl.when(pl.program_id(0) == s)
        def _():
            out[0] = blocks[s][...]


def place(order, blocks, chunk, into):
    rows, width = blocks[0].shape
    extra = [] if into is None else [into]
    return pl.pallas_call(
        place_kernel,
        grid_spec=pltpu.PrefetchScalarGridSpec(
            num_scalar_prefetch=1,
            grid=(4,),
            in_specs=[pl.BlockSpec((rows, width), lambda i, o: (0, 0))] * 4
            + [pl.BlockSpec(memory_space=pl.ANY)] * len(extra),
            out_specs=pl.BlockSpec((1, rows, width), lambda i, o: (o[i], 0, chunk)),
        ),
        out_shape=jax.ShapeDtypeStruct((4, rows, CHUNKS * width), jnp.bfloat16),
        input_output_aliases={5: 0} if extra else {},
        compiler_params=pltpu.CompilerParams(vmem_limit_bytes=VMEM),
    )(order, *blocks, *extra)


def select_kernel(order, *refs):
    blocks, outs = refs[:4], refs[4:]
    for t in DIGITS:
        for s in DIGITS:
            @pl.when(order[t] == s)
            def _():
                outs[t][...] = blocks[s][...]


def select(order, blocks):
    whole = pl.BlockSpec(blocks[0].shape, lambda i, o: (0, 0))
    return pl.pallas_call(
        select_kernel,
        grid_spec=pltpu.PrefetchScalarGridSpec(
            num_scalar_prefetch=1, grid=(1,), in_specs=[whole] * 4, out_specs=[whole] * 4
        ),
        out_shape=[jax.ShapeDtypeStruct(a.shape, a.dtype) for a in blocks],
        compiler_params=pltpu.CompilerParams(vmem_limit_bytes=VMEM),
    )(order, *blocks)


def shift(array, axis, by):
    size = lax.axis_size(axis)
    return lax.ppermute(array, axis, [(i, (i + by) % size) for i in range(size)])


def swap(array):
    return shift(array, "core", 1)


def after(value, *others):
    return lax.optimization_barrier((value,) + others)[0]


BEHIND = (0, 1, 3, 2)
PIECES = tuple((behind, other) for behind in BEHIND for other in (0, 1))


def z_pieces(shard):
    return [shard] + [shift(shard, "zh", behind) for behind in BEHIND[1:]]


def both_cores(pieces):
    return [array for own in pieces for array in (own, swap(own))]


def exchange(blocks, axis):
    return [blocks[0]] + [shift(blocks[s], axis, s) for s in (1, 2, 3)]


def hand_over(shard, axis):
    return lax.all_to_all(shard, axis, 0, 0, tiled=True)


def all_rows(mine):
    return lax.all_gather(mine, ("zh", "core"), axis=2, tiled=True)


def local(coefficients, transfer):
    a, b = lax.axis_index("x"), lax.axis_index("y")
    zh, core = lax.axis_index("zh"), lax.axis_index("core")
    steps = jnp.arange(4, dtype=jnp.int32)

    def order(slots, children):
        head = jnp.stack([core, zh])
        return jnp.concatenate([head, slots % 4, children % 4]).astype(jnp.int32)

    order0 = order(a + steps, steps)
    order1 = order(a + steps, a - steps + 4)
    order2 = order(b + steps, b - steps + 4)
    orders = ((a - b - steps + 8) % 4).astype(jnp.int32)
    orderp = ((b - steps + 4) % 4).astype(jnp.int32)

    pieces = z_pieces(transfer[0])
    first = swap(pieces[0])
    mine1 = hand_over(after(transfer[1], first), "x")
    mine2 = hand_over(after(transfer[2], mine1), "y")
    *near, mine1, mine2 = lax.optimization_barrier((*pieces[1:3], mine1, mine2))
    w0 = [pieces[0], first] + both_cores(near + pieces[3:])
    w1 = all_rows(after(mine1, *near))
    w2 = all_rows(after(mine2, *w0))
    states = [
        exchange(level(order0, w0, [coefficients], PIECES, c, ALL_VMEM), "x") for c in range(CHUNKS)
    ]
    for c in range(CHUNKS):
        memory = VMEM if c else ALL_VMEM
        states[c] = exchange(level(order1, [w1], states[c], vmem=memory), "x")
        states[c] = exchange(select(orders, states[c]), "y")
    for c in range(CHUNKS):
        states[c] = exchange(level(order2, [w2], states[c]), "y")
    result = None
    for c in range(CHUNKS):
        result = place(orderp, states[c], c, result)
    return result


def solution(mesh):
    fine = Mesh(mesh.devices.reshape(2, 4, 4, 4, 2), ("zl", "y", "x", "zh", "core"))
    node, col = ("zl", "y", "x"), ("zh", "core")
    return jax.shard_map(
        local,
        mesh=fine,
        in_specs=(P(node, None, col), P(None, node, None, col, None)),
        out_specs=P(node, None, col),
        check_vma=False,
    )
```

```python
import functools

import jax
import jax.numpy as jnp
from jax import lax
from jax.experimental import pallas as pl
from jax.experimental.pallas import tpu as pltpu
from jax.sharding import Mesh, PartitionSpec as P

DIGITS = range(4)
CHUNKS = 2
VMEM, ALL_VMEM = 20 * 2**20, 60 * 2**20


def assemble(pieces, order, held, weights):
    core, own_zh = order[0], order[1]
    for (behind, other), ref in zip(pieces, held):
        half = 1 - core if other else core
        at = lax.rem(own_zh - behind + 4, 4)
        rows = pl.ds(pl.multiple_of(64 * at + 32 * half, 32), 32)
        weights[:, :, rows, :] = ref[...]


def level_kernel(pieces, order, *refs):
    if pieces:
        held, refs, weights = refs[: len(pieces)], refs[len(pieces) : -1], refs[-1]
        assemble(pieces, order, held, weights)
    else:
        weights, refs = refs[0], refs[1:]
    children, outs = refs[:-4], refs[-4:]
    blocks = [children[0].at[order[6 + p]] for p in DIGITS] if len(children) == 1 else children
    for s in DIGITS:
        total = sum(
            jnp.dot(
                weights[order[2 + s], order[6 + p]],
                blocks[p][...],
                preferred_element_type=jnp.float32,
            )
            for p in DIGITS
        )
        outs[s][...] = total.astype(outs[s].dtype)


def level(order, held, children, pieces=(), chunk=None, vmem=VMEM):
    whole = lambda a: pl.BlockSpec(a.shape, lambda i, o: (0,) * a.ndim)
    operands = list(held) + list(children)
    width = children[0].shape[-1]
    specs = [whole(a) for a in operands]
    if chunk is not None:
        width //= CHUNKS
        specs[-1] = pl.BlockSpec((4, 256, width), lambda i, o: (0, 0, chunk))
    return pl.pallas_call(
        functools.partial(level_kernel, pieces),
        grid_spec=pltpu.PrefetchScalarGridSpec(
            num_scalar_prefetch=1,
            grid=(1,),
            in_specs=specs,
            out_specs=[pl.BlockSpec((256, width), lambda i, o: (0, 0))] * 4,
            scratch_shapes=[pltpu.VMEM((4, 4, 256, 256), jnp.bfloat16)] if pieces else [],
        ),
        out_shape=[jax.ShapeDtypeStruct((256, width), jnp.bfloat16)] * 4,
        cost_estimate=pl.CostEstimate(
            flops=2 * 16 * 256 * 256 * width,
            bytes_accessed=2 * (16 * 256 * 256 + 8 * 256 * width),
            transcendentals=0,
        ),
        compiler_params=pltpu.CompilerParams(vmem_limit_bytes=vmem),
    )(order, *operands)


def place_kernel(order, *refs):
    blocks, out = refs[:4], refs[-1]
    for s in DIGITS:
        @pl.when(pl.program_id(0) == s)
        def _():
            out[0] = blocks[s][...]


def place(order, blocks, chunk, into):
    rows, width = blocks[0].shape
    extra = [] if into is None else [into]
    return pl.pallas_call(
        place_kernel,
        grid_spec=pltpu.PrefetchScalarGridSpec(
            num_scalar_prefetch=1,
            grid=(4,),
            in_specs=[pl.BlockSpec((rows, width), lambda i, o: (0, 0))] * 4
            + [pl.BlockSpec(memory_space=pl.ANY)] * len(extra),
            out_specs=pl.BlockSpec((1, rows, width), lambda i, o: (o[i], 0, chunk)),
        ),
        out_shape=jax.ShapeDtypeStruct((4, rows, CHUNKS * width), jnp.bfloat16),
        input_output_aliases={5: 0} if extra else {},
        compiler_params=pltpu.CompilerParams(vmem_limit_bytes=VMEM),
    )(order, *blocks, *extra)


def select_kernel(order, *refs):
    blocks, outs = refs[:4], refs[4:]
    for t in DIGITS:
        for s in DIGITS:
            @pl.when(order[t] == s)
            def _():
                outs[t][...] = blocks[s][...]


def select(order, blocks):
    whole = pl.BlockSpec(blocks[0].shape, lambda i, o: (0, 0))
    return pl.pallas_call(
        select_kernel,
        grid_spec=pltpu.PrefetchScalarGridSpec(
            num_scalar_prefetch=1, grid=(1,), in_specs=[whole] * 4, out_specs=[whole] * 4
        ),
        out_shape=[jax.ShapeDtypeStruct(a.shape, a.dtype) for a in blocks],
        compiler_params=pltpu.CompilerParams(vmem_limit_bytes=VMEM),
    )(order, *blocks)


def shift(array, axis, by):
    size = lax.axis_size(axis)
    return lax.ppermute(array, axis, [(i, (i + by) % size) for i in range(size)])


def swap(array):
    return shift(array, "core", 1)


def after(value, *others):
    return lax.optimization_barrier((value,) + others)[0]


BEHIND = (0, 1, 3, 2)
PIECES = tuple((behind, other) for behind in BEHIND for other in (0, 1))


def z_pieces(shard):
    return [shard] + [shift(shard, "zh", behind) for behind in BEHIND[1:]]


def both_cores(pieces):
    return [array for own in pieces for array in (own, swap(own))]


def exchange(blocks, axis):
    return [blocks[0]] + [shift(blocks[s], axis, s) for s in (1, 2, 3)]


def hand_over(shards):
    first, second = lax.all_to_all(shards, "y", 1, 1, tiled=True)
    return jnp.stack([lax.all_to_all(first, "x", 0, 0, tiled=True), second])


def all_rows(mine):
    return lax.all_gather(mine, ("zh", "core"), axis=3, tiled=True)


def local(coefficients, transfer):
    a, b = lax.axis_index("x"), lax.axis_index("y")
    zh, core = lax.axis_index("zh"), lax.axis_index("core")
    steps = jnp.arange(4, dtype=jnp.int32)

    def order(slots, children):
        head = jnp.stack([core, zh])
        return jnp.concatenate([head, slots % 4, children % 4]).astype(jnp.int32)

    order0 = order(b + steps, steps)
    orders = ((b - a - steps + 8) % 4).astype(jnp.int32)
    order1 = order(a + steps, a - steps + 4)
    order2 = order(b + steps, a - steps + 4)
    orderp = ((b - steps + 4) % 4).astype(jnp.int32)

    pieces = z_pieces(transfer[0])
    first = swap(pieces[0])
    mine = hand_over(transfer[1:])
    w0 = [pieces[0], first] + both_cores(pieces[1:])
    w1, w2 = all_rows(after(mine, *w0))
    states = []
    for c in range(CHUNKS):
        blocks = exchange(level(order0, w0, [coefficients], PIECES, c, ALL_VMEM), "y")
        states.append(blocks)
    states = [exchange(select(orders, blocks), "x") for blocks in states]
    states = [exchange(level(order1, [w1], blocks), "x") for blocks in states]
    states = [exchange(level(order2, [w2], blocks), "y") for blocks in states]
    result = None
    for c in range(CHUNKS):
        result = place(orderp, states[c], c, result)
    return result


def solution(mesh):
    fine = Mesh(mesh.devices.reshape(2, 4, 4, 4, 2), ("zl", "y", "x", "zh", "core"))
    node, col = ("zl", "y", "x"), ("zh", "core")
    return jax.shard_map(
        local,
        mesh=fine,
        in_specs=(P(node, None, col), P(None, node, None, col, None)),
        out_specs=P(node, None, col),
        check_vma=False,
    )
```

```python
import functools

import jax
import jax.numpy as jnp
from jax import lax
from jax.experimental import pallas as pl
from jax.experimental.pallas import tpu as pltpu
from jax.sharding import Mesh, PartitionSpec as P

DIGITS = range(4)
CHUNKS = 2
VMEM, ALL_VMEM = 20 * 2**20, 60 * 2**20


def assemble(pieces, order, held, weights):
    core, own_zh = order[0], order[1]
    for (behind, other), ref in zip(pieces, held):
        half = 1 - core if other else core
        at = lax.rem(own_zh - behind + 4, 4)
        rows = pl.ds(pl.multiple_of(64 * at + 32 * half, 32), 32)
        weights[:, :, rows, :] = ref[...]


def level_kernel(pieces, order, *refs):
    if pieces:
        held, refs, weights = refs[: len(pieces)], refs[len(pieces) : -1], refs[-1]
        assemble(pieces, order, held, weights)
    else:
        weights, refs = refs[0], refs[1:]
    children, outs = refs[:-4], refs[-4:]
    blocks = [children[0].at[order[6 + p]] for p in DIGITS] if len(children) == 1 else children
    for s in DIGITS:
        total = sum(
            jnp.dot(
                weights[order[2 + s], order[6 + p]],
                blocks[p][...],
                preferred_element_type=jnp.float32,
            )
            for p in DIGITS
        )
        outs[s][...] = total.astype(outs[s].dtype)


def level(order, held, children, pieces=(), chunk=None, vmem=VMEM):
    whole = lambda a: pl.BlockSpec(a.shape, lambda i, o: (0,) * a.ndim)
    operands = list(held) + list(children)
    width = children[0].shape[-1]
    specs = [whole(a) for a in operands]
    if chunk is not None:
        width //= CHUNKS
        specs[-1] = pl.BlockSpec((4, 256, width), lambda i, o: (0, 0, chunk))
    return pl.pallas_call(
        functools.partial(level_kernel, pieces),
        grid_spec=pltpu.PrefetchScalarGridSpec(
            num_scalar_prefetch=1,
            grid=(1,),
            in_specs=specs,
            out_specs=[pl.BlockSpec((256, width), lambda i, o: (0, 0))] * 4,
            scratch_shapes=[pltpu.VMEM((4, 4, 256, 256), jnp.bfloat16)] if pieces else [],
        ),
        out_shape=[jax.ShapeDtypeStruct((256, width), jnp.bfloat16)] * 4,
        cost_estimate=pl.CostEstimate(
            flops=2 * 16 * 256 * 256 * width,
            bytes_accessed=2 * (16 * 256 * 256 + 8 * 256 * width),
            transcendentals=0,
        ),
        compiler_params=pltpu.CompilerParams(vmem_limit_bytes=vmem),
    )(order, *operands)


def last_kernel(skip, order, weights, *refs):
    children, outs = refs[:-2], refs[-2:]
    width = children[0].shape[1]
    for s in range(2):
        for c in range(CHUNKS):
            total = sum(
                jnp.dot(
                    weights[order[2 + skip + s], order[6 + p]],
                    children[4 * c + p][...],
                    preferred_element_type=jnp.float32,
                )
                for p in DIGITS
            )
            outs[s][:, c * width : (c + 1) * width] = total.astype(outs[s].dtype)


def last_level(order, weights, states, skip):
    whole = lambda a: pl.BlockSpec(a.shape, lambda i, o: (0,) * a.ndim)
    operands = [weights] + [block for blocks in states for block in blocks]
    width = CHUNKS * states[0][0].shape[1]
    return pl.pallas_call(
        functools.partial(last_kernel, skip),
        grid_spec=pltpu.PrefetchScalarGridSpec(
            num_scalar_prefetch=1,
            grid=(1,),
            in_specs=[whole(a) for a in operands],
            out_specs=[pl.BlockSpec((256, width), lambda i, o: (0, 0))] * 2,
        ),
        out_shape=[jax.ShapeDtypeStruct((256, width), jnp.bfloat16)] * 2,
        cost_estimate=pl.CostEstimate(
            flops=2 * 8 * 256 * 256 * width,
            bytes_accessed=2 * (8 * 256 * 256 + 6 * 256 * width),
            transcendentals=0,
        ),
        compiler_params=pltpu.CompilerParams(vmem_limit_bytes=VMEM),
    )(order, *operands)


def place_kernel(order, *refs):
    blocks, out = refs[:2], refs[-1]
    for s in range(2):
        @pl.when(pl.program_id(0) == s)
        def _():
            out[0] = blocks[s][...]


def place(order, blocks, into):
    rows, width = blocks[0].shape
    extra = [] if into is None else [into]
    return pl.pallas_call(
        place_kernel,
        grid_spec=pltpu.PrefetchScalarGridSpec(
            num_scalar_prefetch=1,
            grid=(2,),
            in_specs=[pl.BlockSpec((rows, width), lambda i, o: (0, 0))] * 2
            + [pl.BlockSpec(memory_space=pl.ANY)] * len(extra),
            out_specs=pl.BlockSpec((1, rows, width), lambda i, o: (o[i], 0, 0)),
        ),
        out_shape=jax.ShapeDtypeStruct((4, rows, width), jnp.bfloat16),
        input_output_aliases={3: 0} if extra else {},
        compiler_params=pltpu.CompilerParams(vmem_limit_bytes=VMEM),
    )(order, *blocks, *extra)


def select_kernel(order, *refs):
    blocks, outs = refs[:4], refs[4:]
    for t in DIGITS:
        for s in DIGITS:
            @pl.when(order[t] == s)
            def _():
                outs[t][...] = blocks[s][...]


def select(order, blocks):
    whole = pl.BlockSpec(blocks[0].shape, lambda i, o: (0, 0))
    return pl.pallas_call(
        select_kernel,
        grid_spec=pltpu.PrefetchScalarGridSpec(
            num_scalar_prefetch=1, grid=(1,), in_specs=[whole] * 4, out_specs=[whole] * 4
        ),
        out_shape=[jax.ShapeDtypeStruct(a.shape, a.dtype) for a in blocks],
        compiler_params=pltpu.CompilerParams(vmem_limit_bytes=VMEM),
    )(order, *blocks)


def shift(array, axis, by):
    size = lax.axis_size(axis)
    return lax.ppermute(array, axis, [(i, (i + by) % size) for i in range(size)])


def swap(array):
    return shift(array, "core", 1)


def after(value, *others):
    return lax.optimization_barrier((value,) + others)[0]


BEHIND = (0, 1, 3, 2)
PIECES = tuple((behind, other) for behind in BEHIND for other in (0, 1))


def z_pieces(shard):
    return [shard] + [shift(shard, "zh", behind) for behind in BEHIND[1:]]


def both_cores(pieces):
    return [array for own in pieces for array in (own, swap(own))]


def exchange(blocks, axis):
    return [blocks[0]] + [shift(blocks[s], axis, s) for s in (1, 2, 3)]


def hand_over(shards):
    first, second = lax.all_to_all(shards, "y", 1, 1, tiled=True)
    return lax.all_to_all(first, "x", 0, 0, tiled=True), second


def all_rows(mine):
    return lax.all_gather(mine, ("zh", "core"), axis=2, tiled=True)


def local(coefficients, transfer):
    a, b = lax.axis_index("x"), lax.axis_index("y")
    zh, core = lax.axis_index("zh"), lax.axis_index("core")
    steps = jnp.arange(4, dtype=jnp.int32)

    def order(slots, children):
        head = jnp.stack([core, zh])
        return jnp.concatenate([head, slots % 4, children % 4]).astype(jnp.int32)

    order0 = order(b + steps, steps)
    orders = ((b - a - steps + 8) % 4).astype(jnp.int32)
    order1 = order(a + steps, a - steps + 4)
    odd, even = jnp.array([1, 3], jnp.int32), jnp.array([0, 2], jnp.int32)
    order2 = order(b + jnp.concatenate([odd, even]), a - steps + 4)

    pieces = z_pieces(transfer[0])
    first = swap(pieces[0])
    mine1, mine2 = hand_over(transfer[1:])
    *far, mine1 = lax.optimization_barrier((*pieces[1:], mine1))
    w0 = [pieces[0], first] + both_cores(far)
    w1 = all_rows(mine1)
    w2 = all_rows(after(mine2, *w0))
    states = []
    for c in range(CHUNKS):
        blocks = exchange(level(order0, w0, [coefficients], PIECES, c, ALL_VMEM), "y")
        states.append(blocks)
    states = [exchange(select(orders, blocks), "x") for blocks in states]
    states = [exchange(level(order1, [w1], blocks), "x") for blocks in states]
    one, three = last_level(order2, w2, states, 0)
    one, three = shift(one, "y", 1), shift(three, "y", 3)
    own, two = last_level(order2, w2, states, 2)
    two = shift(two, "y", 2)
    result = place((b - odd + 4) % 4, [one, three], None)
    return place((b - even + 4) % 4, [own, two], result)


def solution(mesh):
    fine = Mesh(mesh.devices.reshape(2, 4, 4, 4, 2), ("zl", "y", "x", "zh", "core"))
    node, col = ("zl", "y", "x"), ("zh", "core")
    return jax.shard_map(
        local,
        mesh=fine,
        in_specs=(P(node, None, col), P(None, node, None, col, None)),
        out_specs=P(node, None, col),
        check_vma=False,
    )
```

```python
import functools

import jax
import jax.numpy as jnp
from jax import lax
from jax.experimental import pallas as pl
from jax.experimental.pallas import tpu as pltpu
from jax.sharding import Mesh, PartitionSpec as P

DIGITS = range(4)
CHUNKS = 2
VMEM, ALL_VMEM = 20 * 2**20, 60 * 2**20


def assemble(pieces, order, held, weights):
    core, own_zh = order[0], order[1]
    for (behind, other), ref in zip(pieces, held):
        half = 1 - core if other else core
        at = lax.rem(own_zh - behind + 4, 4)
        rows = pl.ds(pl.multiple_of(64 * at + 32 * half, 32), 32)
        weights[:, :, rows, :] = ref[...]


def level_kernel(pieces, order, *refs):
    if pieces:
        held, refs, weights = refs[: len(pieces)], refs[len(pieces) : -1], refs[-1]
        assemble(pieces, order, held, weights)
    else:
        weights, refs = refs[0], refs[1:]
    children, outs = refs[:-4], refs[-4:]
    blocks = [children[0].at[order[6 + p]] for p in DIGITS] if len(children) == 1 else children
    for s in DIGITS:
        total = sum(
            jnp.dot(
                weights[order[2 + s], order[6 + p]],
                blocks[p][...],
                preferred_element_type=jnp.float32,
            )
            for p in DIGITS
        )
        outs[s][...] = total.astype(outs[s].dtype)


def level(order, held, children, pieces=(), chunk=None, vmem=VMEM):
    whole = lambda a: pl.BlockSpec(a.shape, lambda i, o: (0,) * a.ndim)
    operands = list(held) + list(children)
    width = children[0].shape[-1]
    specs = [whole(a) for a in operands]
    if chunk is not None:
        width //= CHUNKS
        specs[-1] = pl.BlockSpec((4, 256, width), lambda i, o: (0, 0, chunk))
    return pl.pallas_call(
        functools.partial(level_kernel, pieces),
        grid_spec=pltpu.PrefetchScalarGridSpec(
            num_scalar_prefetch=1,
            grid=(1,),
            in_specs=specs,
            out_specs=[pl.BlockSpec((256, width), lambda i, o: (0, 0))] * 4,
            scratch_shapes=[pltpu.VMEM((4, 4, 256, 256), jnp.bfloat16)] if pieces else [],
        ),
        out_shape=[jax.ShapeDtypeStruct((256, width), jnp.bfloat16)] * 4,
        cost_estimate=pl.CostEstimate(
            flops=2 * 16 * 256 * 256 * width,
            bytes_accessed=2 * (16 * 256 * 256 + 8 * 256 * width),
            transcendentals=0,
        ),
        compiler_params=pltpu.CompilerParams(vmem_limit_bytes=vmem),
    )(order, *operands)


def last_kernel(skip, order, weights, *refs):
    children, outs = refs[:-2], refs[-2:]
    width = children[0].shape[1]
    for s in range(2):
        for c in range(CHUNKS):
            total = sum(
                jnp.dot(
                    weights[order[2 + skip + s], order[6 + p]],
                    children[4 * c + p][...],
                    preferred_element_type=jnp.float32,
                )
                for p in DIGITS
            )
            outs[s][:, c * width : (c + 1) * width] = total.astype(outs[s].dtype)


def last_level(order, weights, states, skip):
    whole = lambda a: pl.BlockSpec(a.shape, lambda i, o: (0,) * a.ndim)
    operands = [weights] + [block for blocks in states for block in blocks]
    width = CHUNKS * states[0][0].shape[1]
    return pl.pallas_call(
        functools.partial(last_kernel, skip),
        grid_spec=pltpu.PrefetchScalarGridSpec(
            num_scalar_prefetch=1,
            grid=(1,),
            in_specs=[whole(a) for a in operands],
            out_specs=[pl.BlockSpec((256, width), lambda i, o: (0, 0))] * 2,
        ),
        out_shape=[jax.ShapeDtypeStruct((256, width), jnp.bfloat16)] * 2,
        cost_estimate=pl.CostEstimate(
            flops=2 * 8 * 256 * 256 * width,
            bytes_accessed=2 * (8 * 256 * 256 + 6 * 256 * width),
            transcendentals=0,
        ),
        compiler_params=pltpu.CompilerParams(vmem_limit_bytes=VMEM),
    )(order, *operands)


def place_kernel(order, *refs):
    blocks, out = refs[:2], refs[-1]
    for s in range(2):
        @pl.when(pl.program_id(0) == s)
        def _():
            out[0] = blocks[s][...]


def place(order, blocks, into):
    rows, width = blocks[0].shape
    extra = [] if into is None else [into]
    return pl.pallas_call(
        place_kernel,
        grid_spec=pltpu.PrefetchScalarGridSpec(
            num_scalar_prefetch=1,
            grid=(2,),
            in_specs=[pl.BlockSpec((rows, width), lambda i, o: (0, 0))] * 2
            + [pl.BlockSpec(memory_space=pl.ANY)] * len(extra),
            out_specs=pl.BlockSpec((1, rows, width), lambda i, o: (o[i], 0, 0)),
        ),
        out_shape=jax.ShapeDtypeStruct((4, rows, width), jnp.bfloat16),
        input_output_aliases={3: 0} if extra else {},
        compiler_params=pltpu.CompilerParams(vmem_limit_bytes=VMEM),
    )(order, *blocks, *extra)


def select_kernel(order, *refs):
    blocks, outs = refs[:4], refs[4:]
    for t in DIGITS:
        for s in DIGITS:
            @pl.when(order[t] == s)
            def _():
                outs[t][...] = blocks[s][...]


def select(order, blocks):
    whole = pl.BlockSpec(blocks[0].shape, lambda i, o: (0, 0))
    return pl.pallas_call(
        select_kernel,
        grid_spec=pltpu.PrefetchScalarGridSpec(
            num_scalar_prefetch=1, grid=(1,), in_specs=[whole] * 4, out_specs=[whole] * 4
        ),
        out_shape=[jax.ShapeDtypeStruct(a.shape, a.dtype) for a in blocks],
        compiler_params=pltpu.CompilerParams(vmem_limit_bytes=VMEM),
    )(order, *blocks)


def shift(array, axis, by):
    size = lax.axis_size(axis)
    return lax.ppermute(array, axis, [(i, (i + by) % size) for i in range(size)])


def swap(array):
    return shift(array, "core", 1)


def after(value, *others):
    return lax.optimization_barrier((value,) + others)[0]


BEHIND = (0, 1, 3, 2)
PIECES = tuple((behind, other) for behind in BEHIND for other in (0, 1))


def z_pieces(shard):
    return [shard] + [shift(shard, "zh", behind) for behind in BEHIND[1:]]


def both_cores(pieces):
    return [array for own in pieces for array in (own, swap(own))]


def exchange(blocks, axis):
    return [blocks[0]] + [shift(blocks[s], axis, s) for s in (1, 2, 3)]


def hand_over(shards):
    first, second = lax.all_to_all(shards, "y", 1, 1, tiled=True)
    return lax.all_to_all(first, "x", 0, 0, tiled=True), second


def all_rows(mine):
    return lax.all_gather(mine, ("zh", "core"), axis=2, tiled=True)


def local(coefficients, transfer):
    a, b = lax.axis_index("x"), lax.axis_index("y")
    zh, core = lax.axis_index("zh"), lax.axis_index("core")
    steps = jnp.arange(4, dtype=jnp.int32)

    def order(slots, children):
        head = jnp.stack([core, zh])
        return jnp.concatenate([head, slots % 4, children % 4]).astype(jnp.int32)

    order0 = order(b + steps, steps)
    orders = ((b - a - steps + 8) % 4).astype(jnp.int32)
    order1 = order(a + steps, a - steps + 4)
    odd, even = jnp.array([1, 3], jnp.int32), jnp.array([0, 2], jnp.int32)
    order2 = order(b + jnp.concatenate([odd, even]), a - steps + 4)

    pieces = z_pieces(transfer[0])
    first = swap(pieces[0])
    mine1, mine2 = hand_over(transfer[1:])
    *far, mine1 = lax.optimization_barrier((*pieces[1:], mine1))
    w0 = [pieces[0], first] + both_cores(far)
    w1 = all_rows(mine1)
    w2 = all_rows(after(mine2, *w0))
    states = []
    for c in range(CHUNKS):
        blocks = exchange(level(order0, w0, [coefficients], PIECES, c, VMEM if c else ALL_VMEM), "y")
        states.append(blocks)
    states = [exchange(select(orders, blocks), "x") for blocks in states]
    states = [exchange(level(order1, [w1], blocks), "x") for blocks in states]
    one, three = last_level(order2, w2, states, 0)
    one, three = shift(one, "y", 1), shift(three, "y", 3)
    own, two = last_level(order2, w2, states, 2)
    two = shift(two, "y", 2)
    result = place((b - odd + 4) % 4, [one, three], None)
    return place((b - even + 4) % 4, [own, two], result)


def solution(mesh):
    fine = Mesh(mesh.devices.reshape(2, 4, 4, 4, 2), ("zl", "y", "x", "zh", "core"))
    node, col = ("zl", "y", "x"), ("zh", "core")
    return jax.shard_map(
        local,
        mesh=fine,
        in_specs=(P(node, None, col), P(None, node, None, col, None)),
        out_specs=P(node, None, col),
        check_vma=False,
    )
```
